32 devices in a mesh: dp: 4 (over y, x), seq: 8 (over z, core).
Axes of the slice: x: 2, y: 2, z: 4, core: 2. Of those that a mesh axis runs over, the one named last changes fastest.
Arguments:
- tokens: bfloat16 [4, 1024, 2048], P('dp', 'seq'), may hold values from -6 to 6
- first_gain: bfloat16 [2048], P(('dp', 'seq')), may hold values from 0.5 to 1.5
- query_weight: bfloat16 [2048, 2048], P(('dp', 'seq')), may hold values from -0.125 to 0.125
- key_weight: bfloat16 [2048, 2048], P(('dp', 'seq')), may hold values from -0.125 to 0.125
- value_weight: bfloat16 [2048, 2048], P(('dp', 'seq')), may hold values from -0.125 to 0.125
- out_weight: bfloat16 [2048, 2048], P(('dp', 'seq')), may hold values from -0.75 to 0.75
- second_gain: bfloat16 [2048], P(('dp', 'seq')), may hold values from 0.5 to 1.5
- gate_weight: bfloat16 [2048, 8192], P(('dp', 'seq')), may hold values from -0.125 to 0.125
- up_weight: bfloat16 [2048, 8192], P(('dp', 'seq')), may hold values from -0.125 to 0.125
- down_weight: bfloat16 [2048, 8192], P(('dp', 'seq')), may hold values from -0.0625 to 0.0625
- cotangent: bfloat16 [4, 1024, 2048], P('dp', 'seq'), may hold values from -6 to 6
Outputs:
- output: bfloat16 [4, 1024, 2048], P('dp', 'seq')
- input_grad: bfloat16 [4, 1024, 2048], P('dp', 'seq')
- first_gain_grad: float32 [2048], P(('dp', 'seq'))
- query_weight_grad: float32 [2048, 2048], P(('dp', 'seq'))
- key_weight_grad: float32 [2048, 2048], P(('dp', 'seq'))
- value_weight_grad: float32 [2048, 2048], P(('dp', 'seq'))
- out_weight_grad: float32 [2048, 2048], P(('dp', 'seq'))
- second_gain_grad: float32 [2048], P(('dp', 'seq'))
- gate_weight_grad: float32 [2048, 8192], P(('dp', 'seq'))
- up_weight_grad: float32 [2048, 8192], P(('dp', 'seq'))
- down_weight_grad: float32 [2048, 8192], P(('dp', 'seq'))
The draws below stay inside these ranges and needn't reach their ends.
All inputs are finite; a program needn't handle non-finite values.
Results may differ from the reference program's by a relative error of at most 0.014.
Values may be sent and summed in bfloat16 or wider, within the bound.
No kernel may reach another device: no remote copies, remote signals or barrier semaphores. Data moves between devices by JAX's collectives and lax.ppermute only.
A program may use at most 576 MiB of HBM per device.

```python
import jax
import jax.numpy as jnp
from jax import lax

D = 2048
HEADS = 32
HEAD = 64
FF = 8192
LENGTH = 1024
SEQS = 4


def raised(entries, key, source, target, parts, factor):
    owner, partner = [(jnp.arange(entries.shape[axis_at]) // (entries.shape[axis_at] // parts)).reshape([-1 if axis == axis_at else 1 for axis in range(entries.ndim)]) for axis_at in (source, target)]
    chosen = jax.random.permutation(key, parts)[partner]
    strong = (owner == chosen) | (owner == (partner + parts // 2) % parts)
    return jnp.where(strong, factor * entries, entries)


def block_levels(key, dims, split, smallest, top_value):
    def one(axis_at, shards_of):
        steps = jax.random.uniform(jax.random.fold_in(jax.random.fold_in(key, 6), axis_at), (shards_of,), jnp.float32, smallest / len(split), top_value / len(split))
        return jnp.repeat(jnp.exp(steps), dims[axis_at] // shards_of).reshape((-1,) + (1,) * (len(dims) - axis_at - 1))

    loudness = one(*split[0])
    for cut in split[1:]:
        loudness = loudness * one(*cut)
    return loudness


def normal_values(own_key, extent, width, bound, shards=(), held_as=jnp.bfloat16):
    values = width * jax.random.normal(own_key, extent, jnp.float32)
    if shards:
        values = values * block_levels(own_key, extent, shards, -0.22, 0.18)
    return jnp.clip(values, -bound, bound).astype(held_as)


def bell_draw_with(key, extent, deviation, limit, cuts, heavy, held_as=jnp.bfloat16):
    array = deviation * jax.random.normal(key, extent, jnp.float32)
    if cuts:
        array = array * block_levels(key, extent, cuts, -0.22, 0.18)
    return jnp.clip(raised(array, jax.random.fold_in(key, 3), *heavy), -limit, limit).astype(held_as)


def setup_inputs(seed: int = 0) -> dict:
    arg_keys = jax.random.split(jax.random.key(seed), 12)
    return {
        "tokens": bell_draw_with(arg_keys[0], (SEQS, LENGTH, D), 1.0, 6.0, ((0, 4), (1, 8)), (1, 2, 8, 2.0)),
        "first_gain": jnp.clip(1.0 + 0.1 * jax.random.normal(arg_keys[1], (D,), jnp.float32), 0.5, 1.5).astype(jnp.bfloat16),
        "query_weight": normal_values(arg_keys[2], (D, D), D ** -0.5, 0.125, ((0, 32),)),
        "key_weight": normal_values(arg_keys[3], (D, D), D ** -0.5, 0.125, ((0, 32),)),
        "value_weight": normal_values(arg_keys[4], (D, D), D ** -0.5, 0.125, ((0, 32),)),
        "out_weight": normal_values(arg_keys[5], (D, D), (D // 32) ** -0.5, 0.75, ((0, 32),)),
        "second_gain": jnp.clip(1.0 + 0.1 * jax.random.normal(arg_keys[6], (D,), jnp.float32), 0.5, 1.5).astype(jnp.bfloat16),
        "gate_weight": normal_values(arg_keys[7], (D, FF), D ** -0.5, 0.125, ((0, 32),)),
        "up_weight": normal_values(arg_keys[8], (D, FF), D ** -0.5, 0.125, ((0, 32),)),
        "down_weight": normal_values(arg_keys[9], (D, FF), FF ** -0.5, 0.0625, ((0, 32),)),
        "cotangent": bell_draw_with(arg_keys[10], (SEQS, LENGTH, D), 1.0, 6.0, ((0, 4), (1, 8)), (1, 2, 8, 2.0)),
    }


EPS = 1e-05
THETA = 130000.0
BIG_NEG = -1e+30

@jax.custom_vjp
def low(v):
    return lax.optimization_barrier(v.astype(jnp.bfloat16)).astype(jnp.float32)

@jax.custom_vjp
def low_back(v):
    return v

def low_keep(v):
    return (low(v), None)

def low_pass(kept, grad):
    return (grad,)

def back_keep(v):
    return (v, None)

def back_low(kept, grad):
    return (low(grad),)
low.defvjp(low_keep, low_pass)
low_back.defvjp(back_keep, back_low)

def rope_tables(positions, head_size):
    half_size = head_size // 2
    frequency = THETA ** (-(jnp.arange(half_size, dtype=jnp.float32) * 2.0 / head_size))
    angles = positions.astype(jnp.float32)[:, None] * frequency[None, :]
    angles = jnp.concatenate([angles, angles], axis=1)
    return (jnp.cos(angles), jnp.sin(angles))

def rotate(field_in, cos_table, sin_table):
    row_count = field_in.shape[0]
    split_heads = field_in.reshape(row_count, -1, cos_table.shape[1])
    half_size = cos_table.shape[1] // 2
    turned = jnp.concatenate([-split_heads[:, :, half_size:], split_heads[:, :, :half_size]], axis=2)
    result = split_heads * cos_table[:, None, :] + turned * sin_table[:, None, :]
    return result.reshape(row_count, -1)

def causal_head(query_head, key_head, value_head):
    length = query_head.shape[0]
    product = jnp.dot(query_head, key_head.T, precision=lax.Precision.HIGHEST)
    scores = low_back(HEAD ** (-0.5) * product)
    allowed = jnp.arange(length)[None, :] <= jnp.arange(length)[:, None]
    scores = jnp.where(allowed, scores, BIG_NEG)
    attn_prob = jnp.exp(scores - jax.nn.logsumexp(scores, axis=1, keepdims=True))
    return jnp.dot(low(attn_prob), value_head, precision=lax.Precision.HIGHEST)

def head_step(triple):
    return causal_head(triple[0], triple[1], triple[2])

def split_heads_of(field_in):
    length = field_in.shape[0]
    return field_in.reshape(length, HEADS, HEAD).transpose(1, 0, 2)

def attention(queries, keys_all, values_all):
    length = queries.shape[0]
    outputs = lax.map(jax.checkpoint(head_step), (split_heads_of(queries), split_heads_of(keys_all), split_heads_of(values_all)))
    return outputs.transpose(1, 0, 2).reshape(length, HEADS * HEAD)

def forward(inputs, first_gain, query_weight, key_weight, value_weight, out_weight, second_gain, gate_weight, up_weight, down_weight, cos_table, sin_table):
    precise = lax.Precision.HIGHEST
    inv_first = lax.rsqrt(lax.optimization_barrier(jnp.mean(inputs * inputs, axis=1, keepdims=True)) + EPS)
    normed_first = low(inputs * inv_first * first_gain)
    query_pre = low_back(jnp.dot(normed_first, query_weight, precision=precise))
    key_pre = low_back(jnp.dot(normed_first, key_weight, precision=precise))
    value_low = low_back(low(jnp.dot(normed_first, value_weight, precision=precise)))
    query_rot = low_back(low(rotate(query_pre, cos_table, sin_table)))
    key_rot = low_back(low(rotate(key_pre, cos_table, sin_table)))
    attended = low_back(low(attention(query_rot, key_rot, value_low)))
    hidden_state = inputs + low_back(jnp.dot(attended, out_weight, precision=precise))
    inv_second = lax.rsqrt(lax.optimization_barrier(jnp.mean(hidden_state * hidden_state, axis=1, keepdims=True)) + EPS)
    normed_second = low(hidden_state * inv_second * second_gain)
    gate_pre = low_back(jnp.dot(normed_second, gate_weight, precision=precise))
    up_pre = low_back(jnp.dot(normed_second, up_weight, precision=precise))
    hidden_low = low(jax.nn.silu(gate_pre) * up_pre)
    return hidden_state + low_back(jnp.dot(hidden_low, down_weight.T, precision=precise))

def reference(tokens, first_gain, query_weight, key_weight, value_weight, out_weight, second_gain, gate_weight, up_weight, down_weight, cotangent):
    length = tokens.shape[1]
    cos_table, sin_table = rope_tables(jnp.arange(length), HEAD)
    weights = tuple((matrix.astype(jnp.float32) for matrix in (first_gain, query_weight, key_weight, value_weight, out_weight, second_gain, gate_weight, up_weight, down_weight)))

    def local_forward(*operands):
        return forward(*operands, cos_table, sin_table)

    def per_sequence(totals, pair):
        sequence_in, cotangent_in = pair
        output, pullback = jax.vjp(local_forward, sequence_in.astype(jnp.float32), *weights)
        grads = pullback(cotangent_in.astype(jnp.float32))
        totals = tuple((running + added for running, added in zip(totals, grads[1:])))
        return (totals, (output.astype(jnp.bfloat16), grads[0].astype(jnp.bfloat16)))
    start_totals = tuple((jnp.zeros_like(matrix) for matrix in weights))
    totals, (outputs, input_grads) = lax.scan(per_sequence, start_totals, (tokens, cotangent))
    return (outputs, input_grads, totals[0], totals[1], totals[2], totals[3], totals[4], totals[5], totals[6], totals[7], totals[8])
```

```python
import jax
import jax.numpy as jnp
from jax import lax
from jax.sharding import PartitionSpec as P

HEAD = 64

EPS = 1e-05
THETA = 130000.0
BIG_NEG = -1e30
CORES = 2
LANES = 128


def rope_tables(positions, head_size):
    half_size = head_size // 2
    frequency = THETA ** (-(jnp.arange(half_size, dtype=jnp.float32) * 2.0 / head_size))
    angles = positions.astype(jnp.float32)[:, None] * frequency[None, :]
    angles = jnp.concatenate([angles, angles], axis=1)
    return (jnp.cos(angles), jnp.sin(angles))


def rotate(field_in, cos_table, sin_table):
    row_count = field_in.shape[0]
    split_heads = field_in.reshape(row_count, -1, cos_table.shape[1])
    half_size = cos_table.shape[1] // 2
    turned = jnp.concatenate(
        [-split_heads[:, :, half_size:], split_heads[:, :, :half_size]], axis=2
    )
    result = split_heads * cos_table[:, None, :] + turned * sin_table[:, None, :]
    return result.reshape(row_count, -1)


def rotate_back(gradient, cos_table, sin_table):
    row_count = gradient.shape[0]
    split_heads = gradient.reshape(row_count, -1, cos_table.shape[1])
    half_size = cos_table.shape[1] // 2
    scaled = split_heads * sin_table[:, None, :]
    moved_back = jnp.concatenate([scaled[:, :, half_size:], -scaled[:, :, :half_size]], axis=2)
    return (split_heads * cos_table[:, None, :] + moved_back).reshape(row_count, -1)


def contract_last(left, right):
    return lax.dot_general(
        left, right, (((1,), (1,)), ((), ())), preferred_element_type=jnp.float32
    )


def contract_first(left, right):
    return lax.dot_general(
        left, right, (((0,), (0,)), ((), ())), preferred_element_type=jnp.float32
    )


def matmul(left, right):
    return jnp.dot(left, right, preferred_element_type=jnp.float32)


def block_scores(queries, keys_all, offset, block_rows, score_scale):
    finish = offset + block_rows
    scores = (
        jnp.einsum(
            "qhd,khd->hqk",
            queries[offset:finish],
            keys_all[:finish],
            preferred_element_type=jnp.float32,
        )
        * score_scale
    )
    allowed = jnp.arange(finish)[None, :] <= (offset + jnp.arange(block_rows))[:, None]
    return jnp.where(allowed[None], scores, BIG_NEG)


def attend_forward(stacked, head_size):
    length = stacked.shape[1]
    queries = stacked[0].reshape(length, -1, head_size)
    keys_all = stacked[1].reshape(length, -1, head_size)
    values_all = stacked[2].reshape(length, -1, head_size)
    block_rows = min(512, length)
    score_scale = head_size ** (-0.5)
    outputs = []
    log_sums = []
    for offset in range(0, length, block_rows):
        finish = offset + block_rows
        scores = block_scores(queries, keys_all, offset, block_rows, score_scale)
        highest = jnp.max(scores, axis=2, keepdims=True)
        log_total = highest + jnp.log(jnp.sum(jnp.exp(scores - highest), axis=2, keepdims=True))
        prob_low = jnp.exp(scores - log_total).astype(jnp.bfloat16)
        block_out = jnp.einsum(
            "hqk,khd->qhd", prob_low, values_all[:finish], preferred_element_type=jnp.float32
        )
        outputs.append(block_out.reshape(block_rows, -1))
        log_sums.append(log_total)
    return (jnp.concatenate(outputs, axis=0).astype(jnp.bfloat16), log_sums)


def attend_backward(stacked, grad_heads, log_sums, head_size):
    length = stacked.shape[1]
    queries = stacked[0].reshape(length, -1, head_size)
    keys_all = stacked[1].reshape(length, -1, head_size)
    values_all = stacked[2].reshape(length, -1, head_size)
    grad_split = grad_heads.reshape(length, -1, head_size)
    block_rows = min(512, length)
    score_scale = head_size ** (-0.5)
    key_grad = jnp.zeros(keys_all.shape, jnp.float32)
    value_grad = jnp.zeros(values_all.shape, jnp.float32)
    query_grads = []
    for index_block, offset in enumerate(range(0, length, block_rows)):
        finish = offset + block_rows
        scores = block_scores(queries, keys_all, offset, block_rows, score_scale)
        attn_prob = jnp.exp(scores - log_sums[index_block])
        prob_low = attn_prob.astype(jnp.bfloat16)
        grad_block = grad_split[offset:finish]
        grad_prob = jnp.einsum(
            "qhd,khd->hqk", grad_block, values_all[:finish], preferred_element_type=jnp.float32
        )
        inner_sum = jnp.sum(attn_prob * grad_prob, axis=2, keepdims=True)
        grad_score = (attn_prob * (grad_prob - inner_sum)).astype(jnp.bfloat16)
        query_part = (
            jnp.einsum(
                "hqk,khd->qhd", grad_score, keys_all[:finish], preferred_element_type=jnp.float32
            )
            * score_scale
        )
        query_grads.append(query_part.reshape(block_rows, -1))
        key_part = (
            jnp.einsum(
                "hqk,qhd->khd",
                grad_score,
                queries[offset:finish],
                preferred_element_type=jnp.float32,
            )
            * score_scale
        )
        key_grad = key_grad.at[:finish].add(key_part)
        value_part = jnp.einsum(
            "hqk,qhd->khd", prob_low, grad_block, preferred_element_type=jnp.float32
        )
        value_grad = value_grad.at[:finish].add(value_part)
    query_all = jnp.concatenate(query_grads, axis=0)
    return jnp.stack(
        [query_all, key_grad.reshape(length, -1), value_grad.reshape(length, -1)]
    ).astype(jnp.bfloat16)


class Seq:
    def __init__(self, size):
        self.size = size
        self.chips = size // CORES
        self.index = lax.axis_index("seq")
        self.chip = self.index // CORES
        self.core = self.index % CORES

    def swap(self, block):
        pairs = [(i, i + 1 - 2 * (i % CORES)) for i in range(self.size)]
        return lax.ppermute(block, "seq", pairs)

    def step(self, block):
        pairs = [(i, (i + CORES) % self.size) for i in range(self.size)]
        return lax.ppermute(block, "seq", pairs)

    def gather(self, block):
        rows = block.shape[0]
        whole = jnp.zeros((self.size * rows,) + block.shape[1:], block.dtype)
        for hop in range(self.chips):
            other = self.swap(block)
            source = (self.chip - hop) % self.chips
            place = (source * CORES + self.core) * rows
            other_place = (source * CORES + 1 - self.core) * rows
            zeros = (0,) * (block.ndim - 1)
            whole = lax.dynamic_update_slice(whole, block, (place,) + zeros)
            whole = lax.dynamic_update_slice(whole, other, (other_place,) + zeros)
            if hop < self.chips - 1:
                block = self.step(block)
        return whole

    def scatter_sum(self, part):
        rows = part.shape[0] // self.size
        grid = part.reshape(self.chips, CORES, rows, -1)
        given = lax.dynamic_index_in_dim(grid, 1 - self.core, 1, keepdims=False)
        kept = lax.dynamic_index_in_dim(grid, self.core, 1, keepdims=False)
        taken = self.swap(given.astype(jnp.bfloat16))

        def own(chip):
            return lax.dynamic_index_in_dim(kept, chip, 0, keepdims=False) + (
                lax.dynamic_index_in_dim(taken, chip, 0, keepdims=False).astype(jnp.float32)
            )

        total = own((self.chip - 1) % self.chips)
        for hop in range(1, self.chips):
            arrived = self.step(total.astype(jnp.bfloat16))
            total = arrived.astype(jnp.float32) + own((self.chip - 1 - hop) % self.chips)
        return total


def local(
    tokens,
    first_gain,
    query_weight,
    key_weight,
    value_weight,
    out_weight,
    second_gain,
    gate_weight,
    up_weight,
    down_weight,
    cotangent,
):
    seq_size = lax.axis_size("seq")
    dp_size = lax.axis_size("dp")
    seq = Seq(seq_size)
    row_count, model_width = tokens.shape[1:]
    length = row_count * seq_size
    shard_rows, hidden_width = gate_weight.shape
    hidden_share = hidden_width // seq_size
    share = model_width // seq_size
    whole_heads = shard_rows % HEAD == 0
    groups = dp_size if whole_heads else 1

    def head_split(matrix):
        rows = matrix.shape[0]
        return matrix.reshape(rows, groups, seq_size, -1).transpose(2, 0, 1, 3).reshape(
            seq_size, rows, share
        )

    def head_join(blocks):
        rows = blocks.shape[1]
        return blocks.reshape(seq_size, rows, groups, -1).transpose(1, 2, 0, 3).reshape(
            rows, model_width
        )

    def column_split(matrix):
        rows = matrix.shape[0]
        return matrix.reshape(rows, seq_size, -1).transpose(1, 0, 2)

    gains = jnp.stack([first_gain, second_gain], axis=1)
    gains = jnp.pad(gains, ((0, 0), (0, LANES - 2)))
    gains = jnp.broadcast_to(gains[None], (seq_size,) + gains.shape)
    packed = jnp.concatenate(
        [head_split(query_weight), head_split(key_weight), head_split(value_weight), gains], axis=2
    )
    packed = lax.all_to_all(packed, "seq", split_axis=0, concat_axis=0, tiled=True)
    qkv_all = lax.all_gather(
        packed.reshape(seq_size * shard_rows, -1), "dp", axis=0, tiled=True
    )
    qkv_weight = qkv_all[:, : 3 * share]
    gain_rows = qkv_all[:, 3 * share : 3 * share + 2].astype(jnp.float32).T
    gain_first = gain_rows[0]
    gain_second = gain_rows[1]
    if whole_heads:
        out_share = lax.all_gather(out_weight, "dp", axis=0, tiled=True)
    else:
        out_share = lax.dynamic_slice_in_dim(
            lax.all_gather(out_weight, ("dp", "seq"), axis=0, tiled=True),
            lax.axis_index("seq") * share,
            share,
            axis=0,
        )
    feed = jnp.concatenate(
        [column_split(gate_weight), column_split(up_weight), column_split(down_weight)], axis=2
    )
    feed = lax.all_to_all(feed, "seq", split_axis=0, concat_axis=0, tiled=True)
    feed = lax.all_gather(feed.reshape(seq_size * shard_rows, -1), "dp", axis=0, tiled=True)
    gate_share = feed[:, :hidden_share]
    up_share = feed[:, hidden_share : 2 * hidden_share]
    down_share = feed[:, 2 * hidden_share :]

    inputs = tokens[0].astype(jnp.float32)
    inv_first = lax.rsqrt(jnp.mean(inputs * inputs, axis=1, keepdims=True) + EPS)
    cos_table, sin_table = rope_tables(jnp.arange(length), HEAD)
    tokens_all = seq.gather(tokens[0]).astype(jnp.float32)
    inv_all = lax.rsqrt(jnp.mean(tokens_all * tokens_all, axis=1, keepdims=True) + EPS)
    normed_low = (tokens_all * inv_all * gain_first[None, :]).astype(jnp.bfloat16)
    qkv = matmul(normed_low, qkv_weight)
    stacked = jnp.stack(
        [
            rotate(qkv[:, :share], cos_table, sin_table).astype(jnp.bfloat16),
            rotate(qkv[:, share : 2 * share], cos_table, sin_table).astype(jnp.bfloat16),
            qkv[:, 2 * share :].astype(jnp.bfloat16),
        ]
    )
    attended, log_sums = attend_forward(stacked, HEAD)
    hidden_state = inputs + seq.scatter_sum(matmul(attended, out_share))
    inv_second = lax.rsqrt(jnp.mean(hidden_state * hidden_state, axis=1, keepdims=True) + EPS)
    normed_second = hidden_state * inv_second
    second_low = seq.gather((normed_second * gain_second[None, :]).astype(jnp.bfloat16))
    gate_pre = matmul(second_low, gate_share)
    up_pre = matmul(second_low, up_share)
    sigmoid_gate = jax.nn.sigmoid(gate_pre)
    silu_gate = gate_pre * sigmoid_gate
    hidden_low = (silu_gate * up_pre).astype(jnp.bfloat16)
    cotangent_all = seq.gather(cotangent[0])
    grad_hidden = matmul(cotangent_all, down_share)
    grad_gate_low = (
        grad_hidden * up_pre * (sigmoid_gate * (1.0 + gate_pre * (1.0 - sigmoid_gate)))
    ).astype(jnp.bfloat16)
    grad_up_low = (grad_hidden * silu_gate).astype(jnp.bfloat16)
    grad_second = seq.scatter_sum(
        contract_last(grad_gate_low, gate_share) + contract_last(grad_up_low, up_share)
    )
    result = hidden_state + seq.scatter_sum(contract_last(hidden_low, down_share))
    grad_out = cotangent[0].astype(jnp.float32)
    scaled_second = grad_second * gain_second[None, :]
    second_gain_part = jnp.sum(grad_second * normed_second, axis=0)
    grad_state = (
        grad_out
        + inv_second * scaled_second
        - hidden_state
        * inv_second**3
        * jnp.mean(scaled_second * hidden_state, axis=1, keepdims=True)
    )
    grad_state_all = seq.gather(grad_state.astype(jnp.bfloat16))
    grad_heads = contract_last(grad_state_all, out_share).astype(jnp.bfloat16)
    grad_stacked = attend_backward(stacked, grad_heads, log_sums, HEAD)
    grad_qkv = jnp.concatenate(
        [
            rotate_back(grad_stacked[0].astype(jnp.float32), cos_table, sin_table).astype(
                jnp.bfloat16
            ),
            rotate_back(grad_stacked[1].astype(jnp.float32), cos_table, sin_table).astype(
                jnp.bfloat16
            ),
            grad_stacked[2],
        ],
        axis=1,
    )
    grad_first = seq.scatter_sum(contract_last(grad_qkv, qkv_weight))
    normed_first = inputs * inv_first
    scaled_first = grad_first * gain_first[None, :]
    first_gain_part = jnp.sum(grad_first * normed_first, axis=0)
    grad_input = (
        grad_state
        + inv_first * scaled_first
        - inputs * inv_first**3 * jnp.mean(scaled_first * inputs, axis=1, keepdims=True)
    )

    def rows_to_owner(part):
        mine = lax.psum_scatter(
            part.astype(jnp.bfloat16), "dp", scatter_dimension=0, tiled=True
        )
        mine = mine.reshape(seq_size, shard_rows, -1)
        return lax.all_to_all(mine, "seq", split_axis=0, concat_axis=0, tiled=True)

    feed_grad = rows_to_owner(
        jnp.concatenate(
            [
                contract_first(second_low, grad_gate_low).astype(jnp.bfloat16),
                contract_first(second_low, grad_up_low).astype(jnp.bfloat16),
                contract_first(cotangent_all, hidden_low).astype(jnp.bfloat16),
            ],
            axis=1,
        )
    )
    out_part = contract_first(attended, grad_state_all)
    if whole_heads:
        out_grad = lax.psum_scatter(
            out_part.astype(jnp.bfloat16), "dp", scatter_dimension=0, tiled=True
        )
    else:
        out_grad = lax.psum_scatter(
            lax.dynamic_update_slice(
                jnp.zeros((model_width, model_width), jnp.float32),
                out_part,
                (lax.axis_index("seq") * share, 0),
            ),
            ("dp", "seq"),
            scatter_dimension=0,
            tiled=True,
        )
    gain_part = jnp.stack([first_gain_part, second_gain_part], axis=1)
    gain_part = jnp.pad(gain_part, ((0, 0), (0, LANES - 2)))
    qkv_grad = rows_to_owner(
        jnp.concatenate([contract_first(normed_low, grad_qkv), gain_part], axis=1)
    ).astype(jnp.float32)
    gain_grad = jnp.sum(qkv_grad[:, :, 3 * share : 3 * share + 2], axis=0)

    def feed_join(index):
        blocks = feed_grad[:, :, index * hidden_share : (index + 1) * hidden_share]
        return blocks.transpose(1, 0, 2).reshape(shard_rows, hidden_width).astype(jnp.float32)

    return (
        result.astype(jnp.bfloat16)[None],
        grad_input.astype(jnp.bfloat16)[None],
        gain_grad[:, 0],
        head_join(qkv_grad[:, :, :share]),
        head_join(qkv_grad[:, :, share : 2 * share]),
        head_join(qkv_grad[:, :, 2 * share : 3 * share]),
        out_grad.astype(jnp.float32),
        gain_grad[:, 1],
        feed_join(0),
        feed_join(1),
        feed_join(2),
    )


def solution(mesh):
    in_specs = (
        P("dp", "seq", None),
        P(("dp", "seq")),
        P(("dp", "seq"), None),
        P(("dp", "seq"), None),
        P(("dp", "seq"), None),
        P(("dp", "seq"), None),
        P(("dp", "seq")),
        P(("dp", "seq"), None),
        P(("dp", "seq"), None),
        P(("dp", "seq"), None),
        P("dp", "seq", None),
    )
    out_specs = (
        P("dp", "seq", None),
        P("dp", "seq", None),
        P(("dp", "seq")),
        P(("dp", "seq"), None),
        P(("dp", "seq"), None),
        P(("dp", "seq"), None),
        P(("dp", "seq"), None),
        P(("dp", "seq")),
        P(("dp", "seq"), None),
        P(("dp", "seq"), None),
        P(("dp", "seq"), None),
    )
    return jax.shard_map(local, mesh=mesh, in_specs=in_specs, out_specs=out_specs, check_vma=False)
```

```python
import jax
import jax.numpy as jnp
from jax import lax
from jax.sharding import PartitionSpec as P


HEAD = 64

EPS = 1e-05
THETA = 130000.0
BIG_NEG = -1e30
CORES = 2
LANES = 128


def rope_tables(positions, head_size):
    half_size = head_size // 2
    frequency = THETA ** (-(jnp.arange(half_size, dtype=jnp.float32) * 2.0 / head_size))
    angles = positions.astype(jnp.float32)[:, None] * frequency[None, :]
    angles = jnp.concatenate([angles, angles], axis=1)
    return (jnp.cos(angles), jnp.sin(angles))


def rotate(field_in, cos_table, sin_table):
    row_count = field_in.shape[0]
    split_heads = field_in.reshape(row_count, -1, cos_table.shape[1])
    half_size = cos_table.shape[1] // 2
    turned = jnp.concatenate(
        [-split_heads[:, :, half_size:], split_heads[:, :, :half_size]], axis=2
    )
    result = split_heads * cos_table[:, None, :] + turned * sin_table[:, None, :]
    return result.reshape(row_count, -1)


def rotate_back(gradient, cos_table, sin_table):
    row_count = gradient.shape[0]
    split_heads = gradient.reshape(row_count, -1, cos_table.shape[1])
    half_size = cos_table.shape[1] // 2
    scaled = split_heads * sin_table[:, None, :]
    moved_back = jnp.concatenate([scaled[:, :, half_size:], -scaled[:, :, :half_size]], axis=2)
    return (split_heads * cos_table[:, None, :] + moved_back).reshape(row_count, -1)


def contract_last(left, right):
    return lax.dot_general(
        left, right, (((1,), (1,)), ((), ())), preferred_element_type=jnp.float32
    )


def contract_first(left, right):
    return lax.dot_general(
        left, right, (((0,), (0,)), ((), ())), preferred_element_type=jnp.float32
    )


def matmul(left, right):
    return jnp.dot(left, right, preferred_element_type=jnp.float32)


def block_scores(queries, keys_all, offset, block_rows, score_scale):
    finish = offset + block_rows
    scores = (
        jnp.einsum(
            "qhd,khd->hqk",
            queries[offset:finish],
            keys_all[:finish],
            preferred_element_type=jnp.float32,
        )
        * score_scale
    )
    allowed = jnp.arange(finish)[None, :] <= (offset + jnp.arange(block_rows))[:, None]
    return jnp.where(allowed[None], scores, BIG_NEG)


def attend_forward(stacked, head_size):
    length = stacked.shape[1]
    queries = stacked[0].reshape(length, -1, head_size)
    keys_all = stacked[1].reshape(length, -1, head_size)
    values_all = stacked[2].reshape(length, -1, head_size)
    block_rows = min(512, length)
    score_scale = head_size ** (-0.5)
    outputs = []
    log_sums = []
    for offset in range(0, length, block_rows):
        finish = offset + block_rows
        scores = block_scores(queries, keys_all, offset, block_rows, score_scale)
        highest = jnp.max(scores, axis=2, keepdims=True)
        log_total = highest + jnp.log(jnp.sum(jnp.exp(scores - highest), axis=2, keepdims=True))
        prob_low = jnp.exp(scores - log_total).astype(jnp.bfloat16)
        block_out = jnp.einsum(
            "hqk,khd->qhd", prob_low, values_all[:finish], preferred_element_type=jnp.float32
        )
        outputs.append(block_out.reshape(block_rows, -1))
        log_sums.append(log_total)
    return (jnp.concatenate(outputs, axis=0).astype(jnp.bfloat16), log_sums)


def attend_backward(stacked, grad_heads, log_sums, head_size):
    length = stacked.shape[1]
    queries = stacked[0].reshape(length, -1, head_size)
    keys_all = stacked[1].reshape(length, -1, head_size)
    values_all = stacked[2].reshape(length, -1, head_size)
    grad_split = grad_heads.reshape(length, -1, head_size)
    block_rows = min(512, length)
    score_scale = head_size ** (-0.5)
    key_grad = jnp.zeros(keys_all.shape, jnp.float32)
    value_grad = jnp.zeros(values_all.shape, jnp.float32)
    query_grads = []
    for index_block, offset in enumerate(range(0, length, block_rows)):
        finish = offset + block_rows
        scores = block_scores(queries, keys_all, offset, block_rows, score_scale)
        attn_prob = jnp.exp(scores - log_sums[index_block])
        prob_low = attn_prob.astype(jnp.bfloat16)
        grad_block = grad_split[offset:finish]
        grad_prob = jnp.einsum(
            "qhd,khd->hqk", grad_block, values_all[:finish], preferred_element_type=jnp.float32
        )
        inner_sum = jnp.sum(attn_prob * grad_prob, axis=2, keepdims=True)
        grad_score = (attn_prob * (grad_prob - inner_sum)).astype(jnp.bfloat16)
        query_part = (
            jnp.einsum(
                "hqk,khd->qhd", grad_score, keys_all[:finish], preferred_element_type=jnp.float32
            )
            * score_scale
        )
        query_grads.append(query_part.reshape(block_rows, -1))
        key_part = (
            jnp.einsum(
                "hqk,qhd->khd",
                grad_score,
                queries[offset:finish],
                preferred_element_type=jnp.float32,
            )
            * score_scale
        )
        key_grad = key_grad.at[:finish].add(key_part)
        value_part = jnp.einsum(
            "hqk,qhd->khd", prob_low, grad_block, preferred_element_type=jnp.float32
        )
        value_grad = value_grad.at[:finish].add(value_part)
    query_all = jnp.concatenate(query_grads, axis=0)
    return jnp.stack(
        [query_all, key_grad.reshape(length, -1), value_grad.reshape(length, -1)]
    ).astype(jnp.bfloat16)


def after(first, then):
    return lax.optimization_barrier((first, then))[1]


def exchange(blocks):
    return lax.all_to_all(blocks, "seq", split_axis=0, concat_axis=0, tiled=True)


def dp_gather(block):
    return lax.all_gather(block, "dp", axis=0, tiled=True)


def dp_direct_gather(block):
    size = lax.axis_size("dp")
    if size & (size - 1):
        return dp_gather(block)
    mine = lax.axis_index("dp")
    rows = block.shape[0]
    whole = jnp.zeros((size * rows,) + block.shape[1:], block.dtype)
    whole = lax.dynamic_update_slice(whole, block, (mine * rows, 0))
    for turn in range(1, size):
        other = lax.ppermute(block, "dp", [(i, i ^ turn) for i in range(size)])
        whole = lax.dynamic_update_slice(whole, other, ((mine ^ turn) * rows, 0))
    return whole


def dp_sum(part):
    return lax.psum_scatter(part, "dp", scatter_dimension=0, tiled=True)


class Seq:
    def __init__(self, size):
        self.size = size
        self.chips = size // CORES
        self.index = lax.axis_index("seq")
        self.chip = self.index // CORES
        self.core = self.index % CORES

    def swap(self, block):
        pairs = [(i, i + 1 - 2 * (i % CORES)) for i in range(self.size)]
        return lax.ppermute(block, "seq", pairs)

    def step(self, block):
        pairs = [(i, (i + CORES) % self.size) for i in range(self.size)]
        return lax.ppermute(block, "seq", pairs)

    def gather(self, block):
        rows = block.shape[0]
        return self.gather_into([self.empty(block)], [(0, rows, 0)], block)[0]

    def empty(self, block):
        return jnp.zeros((self.size * block.shape[0],) + block.shape[1:], block.dtype)

    def gather_into(self, wholes, parts, block):
        ends = [start for start, _, _ in parts[1:]] + [block.shape[0]]

        def write(wholes, moved, device):
            return [
                lax.dynamic_update_slice(whole, moved[start:end], (device * stride + shift, 0))
                for whole, (start, stride, shift), end in zip(wholes, parts, ends)
            ]

        for hop in range(self.chips):
            other = self.swap(block)
            source = (self.chip - hop) % self.chips
            wholes = write(wholes, block, source * CORES + self.core)
            wholes = write(wholes, other, source * CORES + 1 - self.core)
            if hop < self.chips - 1:
                block = self.step(block)
        return wholes

    def scatter_sum(self, part, chunks=1):
        rows = part.shape[0] // (self.size * chunks)
        grid = part.reshape(chunks, self.chips, CORES, rows, -1)
        given = lax.dynamic_index_in_dim(grid, 1 - self.core, 2, keepdims=False)
        kept = lax.dynamic_index_in_dim(grid, self.core, 2, keepdims=False)
        taken = self.swap(given.astype(jnp.bfloat16))

        def own(chip):
            total = lax.dynamic_index_in_dim(kept, chip, 1, keepdims=False) + (
                lax.dynamic_index_in_dim(taken, chip, 1, keepdims=False).astype(jnp.float32)
            )
            return total.reshape(chunks * rows, -1)

        total = own((self.chip - 1) % self.chips)
        for hop in range(1, self.chips):
            arrived = self.step(total.astype(jnp.bfloat16))
            total = arrived.astype(jnp.float32) + own((self.chip - 1 - hop) % self.chips)
        return total


def layer(
    tokens,
    first_gain,
    query_weight,
    key_weight,
    value_weight,
    out_weight,
    second_gain,
    gate_weight,
    up_weight,
    down_weight,
    cotangent,
):
    seq_size = lax.axis_size("seq")
    dp_size = lax.axis_size("dp")
    seq = Seq(seq_size)
    row_count, model_width = tokens.shape[1:]
    length = row_count * seq_size
    shard_rows, hidden_width = gate_weight.shape
    hidden_share = hidden_width // seq_size
    share = model_width // seq_size
    whole_heads = shard_rows % HEAD == 0
    groups = dp_size if whole_heads else 1

    def head_split(matrix):
        rows = matrix.shape[0]
        return matrix.reshape(rows, groups, seq_size, -1).transpose(2, 0, 1, 3).reshape(
            seq_size, rows, share
        )

    def head_join(blocks):
        rows = blocks.shape[1]
        return blocks.reshape(seq_size, rows, groups, -1).transpose(1, 2, 0, 3).reshape(
            rows, model_width
        )

    def column_split(matrix):
        rows = matrix.shape[0]
        return matrix.reshape(rows, seq_size, -1).transpose(1, 0, 2)

    gains = jnp.stack([first_gain, second_gain], axis=1)
    gains = jnp.pad(gains, ((0, 0), (0, LANES - 2)))
    gains = jnp.broadcast_to(gains[None], (seq_size,) + gains.shape)
    packed = jnp.concatenate(
        [head_split(query_weight), head_split(key_weight), head_split(value_weight), gains], axis=2
    )
    packed = exchange(packed)
    qkv_all = dp_gather(packed.reshape(seq_size * shard_rows, -1))
    qkv_weight = qkv_all[:, : 3 * share]
    gain_rows = qkv_all[:, 3 * share : 3 * share + 2].astype(jnp.float32).T
    gain_first = gain_rows[0]
    gain_second = gain_rows[1]
    if whole_heads:
        out_share = dp_gather(out_weight)
    else:
        out_share = lax.dynamic_slice_in_dim(
            lax.all_gather(out_weight, ("dp", "seq"), axis=0, tiled=True),
            lax.axis_index("seq") * share,
            share,
            axis=0,
        )
    inputs = tokens[0].astype(jnp.float32)
    inv_first = lax.rsqrt(jnp.mean(inputs * inputs, axis=1, keepdims=True) + EPS)
    cos_table, sin_table = rope_tables(jnp.arange(length), HEAD)
    tokens_all = seq.gather(tokens[0])
    gate_up = after(
        packed, jnp.concatenate([column_split(gate_weight), column_split(up_weight)], axis=2)
    )
    gate_up = exchange(gate_up)
    tokens_all = tokens_all.astype(jnp.float32)
    inv_all = lax.rsqrt(jnp.mean(tokens_all * tokens_all, axis=1, keepdims=True) + EPS)
    normed_low = (tokens_all * inv_all * gain_first[None, :]).astype(jnp.bfloat16)
    qkv = matmul(normed_low, qkv_weight)
    stacked = jnp.stack(
        [
            rotate(qkv[:, :share], cos_table, sin_table).astype(jnp.bfloat16),
            rotate(qkv[:, share : 2 * share], cos_table, sin_table).astype(jnp.bfloat16),
            qkv[:, 2 * share :].astype(jnp.bfloat16),
        ]
    )
    attended, log_sums = attend_forward(stacked, HEAD)
    down = after(tokens_all, column_split(down_weight))
    down = exchange(down)
    gate_up = dp_gather(gate_up.reshape(seq_size * shard_rows, -1))
    down_share = dp_direct_gather(down.reshape(seq_size * shard_rows, -1))
    hidden_state = inputs + seq.scatter_sum(matmul(attended, out_share))
    inv_second = lax.rsqrt(jnp.mean(hidden_state * hidden_state, axis=1, keepdims=True) + EPS)
    normed_second = hidden_state * inv_second
    grad_out = cotangent[0].astype(jnp.float32)
    second_own = (normed_second * gain_second[None, :]).astype(jnp.bfloat16)
    chunks = 2 if row_count % 32 == 0 else 1
    rows = row_count // chunks

    def feed(chunk, before):
        own = slice(chunk * rows, (chunk + 1) * rows)
        block = jnp.concatenate([second_own[own], cotangent[0][own]], axis=0)
        second_low, cotangent_low = seq.gather_into(
            [seq.empty(block[:rows]), seq.empty(block[rows:])],
            [(0, rows, 0), (rows, rows, 0)],
            block,
        )
        pre = matmul(second_low, gate_up)
        gate_pre = pre[:, :hidden_share]
        up_pre = pre[:, hidden_share:]
        sigmoid_gate = jax.nn.sigmoid(gate_pre)
        silu_gate = gate_pre * sigmoid_gate
        hidden_low = (silu_gate * up_pre).astype(jnp.bfloat16)
        grad_hidden = matmul(cotangent_low, down_share)
        grad_gate = grad_hidden * up_pre * (sigmoid_gate * (1.0 + gate_pre * (1.0 - sigmoid_gate)))
        grad_up = grad_hidden * silu_gate
        grad_pre = jnp.concatenate(
            [grad_gate.astype(jnp.bfloat16), grad_up.astype(jnp.bfloat16)], axis=1
        )
        part = contract_last(grad_pre, gate_up)
        grad_second = seq.scatter_sum(part)
        if before is not None:
            grad_second = after(before[1], grad_second)
        scaled_second = grad_second * gain_second[None, :]
        state = hidden_state[own]
        inverse = inv_second[own]
        grad_state = (
            grad_out[own]
            + inverse * scaled_second
            - state * inverse**3 * jnp.mean(scaled_second * state, axis=1, keepdims=True)
        )
        return lax.optimization_barrier(
            (second_low, cotangent_low, hidden_low, grad_pre)
        ), lax.optimization_barrier((grad_state, grad_state.astype(jnp.bfloat16)))

    fed = []
    for chunk in range(chunks):
        fed.append(feed(chunk, fed[-1][1] if fed else None))
    grad_state_all = seq.empty(second_own)
    for chunk in range(chunks):
        grad_state_all = seq.gather_into(
            [grad_state_all], [(0, row_count, chunk * rows)], fed[chunk][1][1]
        )[0]
    grad_state = jnp.concatenate([piece[1][0] for piece in fed], axis=0)
    second_low, cotangent_all, hidden_low, grad_pre = lax.optimization_barrier(
        tuple(
            jnp.concatenate([piece[0][field] for piece in fed], axis=0) for field in range(4)
        )
    )
    down_part = contract_first(cotangent_all, hidden_low).astype(jnp.bfloat16)
    gate_up_part = contract_first(second_low, grad_pre).astype(jnp.bfloat16)
    result = after(grad_state_all, hidden_state) + seq.scatter_sum(
        contract_last(hidden_low, down_share), chunks
    )
    grad_heads = contract_last(grad_state_all, out_share).astype(jnp.bfloat16)
    grad_stacked = attend_backward(stacked, grad_heads, log_sums, HEAD)
    grad_qkv = jnp.concatenate(
        [
            rotate_back(grad_stacked[0].astype(jnp.float32), cos_table, sin_table).astype(
                jnp.bfloat16
            ),
            rotate_back(grad_stacked[1].astype(jnp.float32), cos_table, sin_table).astype(
                jnp.bfloat16
            ),
            grad_stacked[2],
        ],
        axis=1,
    )
    grad_first = seq.scatter_sum(contract_last(grad_qkv, qkv_weight))
    scaled_first = grad_first * gain_first[None, :]
    grad_input = (
        grad_state
        + inv_first * scaled_first
        - inputs * inv_first**3 * jnp.mean(scaled_first * inputs, axis=1, keepdims=True)
    )

    def rows_to_owner(part):
        return exchange(part.reshape(seq_size, shard_rows, -1))

    down_mine = dp_sum(down_part)
    gate_up_mine = dp_sum(gate_up_part)
    down_grad = rows_to_owner(down_mine)
    gate_up_grad = rows_to_owner(gate_up_mine)
    out_part = contract_first(attended, grad_state_all)
    if whole_heads:
        out_grad = dp_sum(out_part.astype(jnp.bfloat16))
    else:
        out_grad = lax.psum_scatter(
            lax.dynamic_update_slice(
                jnp.zeros((model_width, model_width), jnp.float32),
                out_part,
                (lax.axis_index("seq") * share, 0),
            ),
            ("dp", "seq"),
            scatter_dimension=0,
            tiled=True,
        )
    qkv_part = contract_first(normed_low, grad_qkv)
    qkv_grad = rows_to_owner(dp_sum(qkv_part.astype(jnp.bfloat16))).astype(jnp.float32)

    def feed_join(blocks):
        return blocks.transpose(1, 0, 2).reshape(shard_rows, hidden_width).astype(jnp.float32)

    query_grad = head_join(qkv_grad[:, :, :share])
    key_grad = head_join(qkv_grad[:, :, share : 2 * share])
    value_grad = head_join(qkv_grad[:, :, 2 * share :])
    gate_grad = feed_join(gate_up_grad[:, :, :hidden_share])
    up_grad = feed_join(gate_up_grad[:, :, hidden_share:])

    def gain_grad(gain, *matrices):
        total = sum(jnp.sum(matrix.astype(jnp.float32) * grad, axis=1) for matrix, grad in matrices)
        return total / gain.astype(jnp.float32)

    return (
        result.astype(jnp.bfloat16)[None],
        grad_input.astype(jnp.bfloat16)[None],
        gain_grad(
            first_gain,
            (query_weight, query_grad),
            (key_weight, key_grad),
            (value_weight, value_grad),
        ),
        query_grad,
        key_grad,
        value_grad,
        out_grad.astype(jnp.float32),
        gain_grad(second_gain, (gate_weight, gate_grad), (up_weight, up_grad)),
        gate_grad,
        up_grad,
        feed_join(down_grad),
    )


def solution(mesh):
    in_specs = (
        P("dp", "seq", None),
        P(("dp", "seq")),
        P(("dp", "seq"), None),
        P(("dp", "seq"), None),
        P(("dp", "seq"), None),
        P(("dp", "seq"), None),
        P(("dp", "seq")),
        P(("dp", "seq"), None),
        P(("dp", "seq"), None),
        P(("dp", "seq"), None),
        P("dp", "seq", None),
    )
    out_specs = (
        P("dp", "seq", None),
        P("dp", "seq", None),
        P(("dp", "seq")),
        P(("dp", "seq"), None),
        P(("dp", "seq"), None),
        P(("dp", "seq"), None),
        P(("dp", "seq"), None),
        P(("dp", "seq")),
        P(("dp", "seq"), None),
        P(("dp", "seq"), None),
        P(("dp", "seq"), None),
    )
    return jax.shard_map(layer, mesh=mesh, in_specs=in_specs, out_specs=out_specs, check_vma=False)
```
